32 devices in a mesh: rows: 8 (over z, x), rep: 4 (over y, core).
Axes of the slice: x: 2, y: 2, z: 4, core: 2. Of those that a mesh axis runs over, the one named last changes fastest.
Arguments:
- right_side: float32 [32768, 1024], P(('rep', 'rows')), parts along dimension 0, may hold values from -6 to 6
- leaf_inverse: float32 [32768, 256], P(('rep', 'rows')), parts along dimension 0, may hold values from -0.375 to 0.375
- left_factors: float32 [5, 32768, 64], P(None, ('rep', 'rows')), parts along dimension 1, may hold values from -0.75 to 0.75
- right_factors: float32 [5, 32768, 64], P(None, ('rep', 'rows')), parts along dimension 1, may hold values from -0.4375 to 0.4375, as said below
- cores: float32 [124, 128, 128], P('rep'), parts along dimension 0, may hold values from -0.5 to 0.5
Outputs:
- solution: float32 [32768, 1024], P(('rep', 'rows')), parts along dimension 0
The draws below stay inside these ranges and needn't reach their ends.
There are 4 independent parts, one for each index of `rep`. The reference program is written for one: setup_inputs(seed, part) draws one part's arguments, and reference() takes and returns one part's arrays. A program takes and returns all parts, laid end to end along the dimension named above; each array names one. Nothing has to cross between parts.
Inputs may be any that keep to these rules, and one draw needn't show every extreme that they name: `right_factors`: level j's entries are of order (8192 / 2^(j+1))^(-1/2).
All inputs are finite; a program needn't handle non-finite values.
Results may differ from the reference program's by a relative error of at most 0.00016.
Values sent between devices are 32-bit elements; how exact they have to be, the bound alone decides.
A program may use at most 128 MiB of HBM per device.

```python
import jax
import jax.numpy as jnp
from jax import lax

COLS = 1024
RANK = 64
LEVELS = 5
NTOT = 8192
LEAF = 256
NODES = 31


def draw_right_factors(key, part):
    depth = jnp.arange(LEVELS).astype(jnp.float32)
    scale = (NTOT / 2.0 ** (depth + 1.0)) ** (-0.5)
    normal = jax.random.truncated_normal(key, -6.0, 6.0, (LEVELS, NTOT, RANK), jnp.float32)
    return normal * scale[:, None, None]


def steps_of(key, extent, cuts, smallest, largest):
    def one(dim, blocks):
        heights = jax.random.uniform(jax.random.fold_in(jax.random.fold_in(key, 6), dim), (blocks,), jnp.float32, smallest / len(cuts), largest / len(cuts))
        return jnp.repeat(jnp.exp(heights), extent[dim] // blocks).reshape((-1,) + (1,) * (len(extent) - dim - 1))

    level = one(*cuts[0])
    for cut in cuts[1:]:
        level = level * one(*cut)
    return level


def normal_values(stream_key, dims, deviation, limit, cuts=(), kind=jnp.bfloat16):
    drawn = jax.random.normal(stream_key, dims, jnp.float32) * deviation
    if len(cuts) > 0:
        drawn = steps_of(stream_key, dims, cuts, -0.22, 0.18) * drawn
    return jnp.clip(drawn, min=-limit, max=limit).astype(kind)


def setup_inputs(seed: int = 0, part: int = 0) -> dict:
    key_list = jax.random.split(jax.random.key(seed), 6)
    own_keys = jax.random.split(jax.random.fold_in(key_list[5], part), 6)
    right_side = normal_values(own_keys[0], (NTOT, COLS), 1.0, 6.0, ((0, 8),), jnp.float32)
    leaf_inverse = normal_values(own_keys[1], (NTOT, LEAF), LEAF ** -0.5, 0.375, ((0, 8),), jnp.float32)
    left_factors = normal_values(own_keys[2], (LEVELS, NTOT, RANK), RANK ** -0.5, 0.75, ((1, 8),), jnp.float32)
    right_factors = draw_right_factors(jax.random.fold_in(jax.random.fold_in(key_list[5], part), 71), part)
    cores = normal_values(own_keys[4], (NODES, 2 * RANK, 2 * RANK), (2 * RANK) ** -0.5, 0.5, (), jnp.float32)
    return dict(right_side=right_side, leaf_inverse=leaf_inverse, left_factors=left_factors, right_factors=right_factors, cores=cores)


HIGH = lax.Precision.HIGHEST


def reference(right_side, leaf_inverse, left_factors, right_factors, cores):
    blocks = NTOT // LEAF
    solved = jnp.einsum("bij,bjk->bik", leaf_inverse.reshape(blocks, LEAF, LEAF), right_side.reshape(blocks, LEAF, COLS), precision=HIGH).reshape(NTOT, COLS)
    for level in reversed(range(LEVELS)):
        nodes = 2 ** level
        half = NTOT // nodes // 2
        shaped = solved.reshape(nodes, 2, half, COLS)
        basis_v = right_factors[level].reshape(nodes, 2, half, RANK)
        basis_u = left_factors[level].reshape(nodes, 2, half, RANK)
        projected = jnp.einsum("nchr,nchk->ncrk", basis_v, shaped, precision=HIGH)
        stacked = jnp.concatenate([projected[:, 1], projected[:, 0]], axis=1)
        core_set = cores[nodes - 1: 2 * nodes - 1]
        image = jnp.einsum("nst,ntk->nsk", core_set, stacked, precision=HIGH).reshape(nodes, 2, RANK, COLS)
        update = jnp.einsum("nchr,ncrk->nchk", basis_u, image, precision=HIGH)
        solved = (shaped - update).reshape(NTOT, COLS)
    return solved
```

```python
import functools

import jax
import jax.numpy as jnp
from jax import lax
from jax.experimental import pallas as pl
from jax.experimental.pallas import tpu as pltpu
from jax.sharding import PartitionSpec as P

LANES = 128
CHUNK = 2 * LANES
HIGH = lax.Precision.HIGH
F32 = jnp.float32


def dot(a, b):
    return jnp.dot(a, b, precision=HIGH, preferred_element_type=F32)


def dot_nt(a, b):
    return lax.dot_general(
        a, b, (((1,), (1,)), ((), ())), precision=HIGH, preferred_element_type=F32
    )


def split(x):
    high = x.astype(jnp.bfloat16)
    return high, (x - high.astype(F32)).astype(jnp.bfloat16)


def level_order(bits, levels):
    return [bits - 1 - s for s in range(bits)] + list(range(bits, levels))


def local_offset(level, bits, rank):
    return rank * (2 ** (level - bits + 1) - 2)


def tree_kernel(bits, levels, blocks, right_hbm, leaf_hbm, vt_ref, ut_ref, cores_hbm, *refs):
    local_levels = list(range(bits, levels))
    refs = list(refs)
    qg_ref = refs.pop(0)
    ql_ref = refs.pop(0) if local_levels else None
    rbuf, leaf, core_g, m_ref, sem_in = refs[:5]
    gram_out, gram_in, first_out, first_in, later_out, later_in, q_out, q_in, qfull = refs[5:14]
    gram_sem, first_sem, later_sem, q_sem = refs[14:18]
    core_l = refs[18 : 18 + len(local_levels)]
    ch_refs = refs[18 + len(local_levels) :]

    me = lax.axis_index("rows")
    rows_dev = vt_ref.shape[2]
    rank = vt_ref.shape[1]
    chunks = rbuf.shape[0]
    lf = rows_dev // blocks
    upper = lax.rem(me, 2) == 1
    order = level_order(bits, levels)

    def child(s):
        return lax.rem(me // 2**s, 2)

    def partner(s):
        return me + (1 - 2 * child(s)) * 2**s

    loads = []
    slot = 0

    def load(src, dst):
        nonlocal slot
        copy = pltpu.make_async_copy(src, dst, sem_in.at[slot])
        slot += 1
        copy.start()
        return copy

    loads.append(load(leaf_hbm, leaf))
    for s in range(bits):
        level = bits - 1 - s
        loads.append(load(cores_hbm.at[2**level - 1 + me // 2 ** (s + 1)], core_g.at[s]))
    for n, level in enumerate(local_levels):
        count = 2 ** (level - bits)
        loads.append(load(cores_hbm.at[pl.ds(2**level - 1 + me * count, count)], core_l[n]))
    right_loads = [
        load(right_hbm.at[:, pl.ds(c * CHUNK, CHUNK)], rbuf.at[c]) for c in range(chunks)
    ]

    barrier = pltpu.get_barrier_semaphore()
    for s in range(bits):
        pl.semaphore_signal(
            barrier, inc=1, device_id={"rows": partner(s)}, device_id_type=pl.DeviceIdType.MESH
        )
    pl.semaphore_wait(barrier, bits)

    sent = []

    def send(src, dst, sems, s):
        copy = pltpu.make_async_remote_copy(
            src_ref=src,
            dst_ref=dst,
            send_sem=sems.at[0],
            recv_sem=sems.at[1],
            device_id={"rows": partner(s)},
            device_id_type=pl.DeviceIdType.MESH,
        )
        copy.start()
        sent.append(copy)
        return copy

    gram_cols = gram_out.shape[2]
    u_rows = [ut_ref[bits - 1 - s] for s in range(bits - 1)]
    pad = gram_cols - rank * (bits - 1)
    if pad:
        u_rows.append(jnp.zeros((pad, rows_dev), F32))
    v_rows = [vt_ref[bits - 1 - s] for s in range(1, bits)]
    gram_out[0] = dot_nt(jnp.concatenate(v_rows, 0), jnp.concatenate(u_rows, 0))
    gram_copy = {0: send(gram_out.at[0], gram_in.at[0], gram_sem.at[0], 0)}

    for copy in loads:
        copy.wait()
    vt_all = jnp.concatenate([vt_ref[level] for level in order], 0)
    for i in range(blocks):
        cols = slice(i * lf, (i + 1) * lf)
        m_ref[i] = dot(vt_all[:, cols], leaf[cols, :])
    for n, level in enumerate(local_levels):
        count = 2 ** (level - bits)
        node = rows_dev // count
        half = node // 2
        zero = jnp.zeros((rank, half), F32)
        for k in range(count):
            base = k * node
            u_a = ut_ref[level, :, base : base + half]
            u_b = ut_ref[level, :, base + half : base + node]
            diag = jnp.concatenate(
                [jnp.concatenate([u_a, zero], 1), jnp.concatenate([zero, u_b], 1)], 0
            )
            gram = dot_nt(vt_all[: rank * level, base : base + node], diag)
            core = core_l[n][k]
            ch_refs[n][k, : 2 * rank] = core
            ch_refs[n][k, 2 * rank :] = dot(gram, core)

    first_copy, later_copy, q_copy = {}, {}, {}

    def forward(c):
        right_loads[c].wait()
        parts = [dot(m_ref[i], rbuf[c, i * lf : (i + 1) * lf, :]) for i in range(blocks)]
        for n in reversed(range(len(local_levels))):
            level = local_levels[n]
            top = rank * level
            merged = []
            for k in range(len(parts) // 2):
                a, b = parts[2 * k], parts[2 * k + 1]
                image = dot(ch_refs[n][k], jnp.concatenate([b[top:], a[top:]], 0))
                start = local_offset(level, bits, rank) + 2 * rank * k
                ql_ref[start : start + 2 * rank, c * CHUNK : (c + 1) * CHUNK] = image[: 2 * rank]
                merged.append(a[:top] + b[:top] - image[2 * rank :])
            parts = merged
        p = parts[0]
        low, high = p[:, :LANES], p[:, LANES:]
        first_out[c, :rank] = low[:rank]
        first_out[c, rank : 2 * rank] = high[:rank]
        first_out[c, 2 * rank :] = jnp.where(upper, low[rank:], high[rank:])
        first_copy[c] = send(first_out.at[c], first_in.at[c], first_sem.at[c], 0)
        later_out[0, c] = jnp.where(upper, high[rank:], low[rank:])

    def stack(mine, theirs, s):
        first = child(s) == 0
        return jnp.concatenate([jnp.where(first, theirs, mine), jnp.where(first, mine, theirs)], 0)

    def pick(image, s):
        first = child(s) == 0
        return (
            jnp.where(first, image[:rank], image[rank:]),
            jnp.where(first, image[rank:], image[:rank]),
        )

    def correction(s, own, sib):
        zeros = [jnp.zeros((rank, LANES), F32)]
        before, after = s, gram_cols // rank - 1 - s
        rows = slice(rank * s, None)
        q_own = jnp.concatenate(zeros * before + [own] + zeros * after, 0)
        q_sib = jnp.concatenate(zeros * before + [sib] + zeros * after, 0)
        return dot(gram_out[s, rows, :], q_own) + dot(gram_in[s, rows, :], q_sib)

    def grams(s):
        gram_copy[s].wait_recv()
        if s + 1 < bits - 1:
            gram_out[s + 1] = gram_out[s] + gram_in[s]
            gram_copy[s + 1] = send(
                gram_out.at[s + 1], gram_in.at[s + 1], gram_sem.at[s + 1], s + 1
            )

    def step(s, c):
        if c == 0 and s < bits - 1:
            grams(s)
        if s == 0:
            first_copy[c].wait_recv()
            mine = jnp.concatenate([first_out[c, :rank], first_out[c, rank : 2 * rank]], 1)
            theirs = jnp.concatenate([first_in[c, :rank], first_in[c, rank : 2 * rank]], 1)
            image = dot(core_g[0], stack(mine, theirs, 0))
            own, sib = pick(image, 0)
            qfull[0, :, c * CHUNK : (c + 1) * CHUNK] = own
            own = jnp.where(upper, own[:, LANES:], own[:, :LANES])
            sib = jnp.where(upper, sib[:, LANES:], sib[:, :LANES])
            rest = later_out[0, c] + first_in[c, 2 * rank :]
        else:
            later_copy[s, c].wait_recv()
            live = slice(rank * (s - 1), rank * s)
            image = dot(core_g[s], stack(later_out[s, c, live], later_in[s, c, live], s))
            own, sib = pick(image, s)
            q_out[s - 1, c] = own
            q_copy[s, c] = send(q_out.at[s - 1, c], q_in.at[s - 1, c], q_sem.at[s - 1, c], 0)
            if s < bits - 1:
                rest = later_out[s, c, rank * s :] + later_in[s, c, rank * s :]
        if s < bits - 1:
            later_out[s + 1, c, rank * s :] = rest - correction(s, own, sib)
            later_copy[s + 1, c] = send(
                later_out.at[s + 1, c, pl.ds(rank * s, rank * (bits - 1 - s))],
                later_in.at[s + 1, c, pl.ds(rank * s, rank * (bits - 1 - s))],
                later_sem.at[s, c],
                s + 1,
            )

    def finish(s, c):
        q_copy[s, c].wait_recv()
        own, other = q_out[s - 1, c], q_in[s - 1, c]
        qfull[s, :, c * CHUNK : c * CHUNK + LANES] = jnp.where(upper, other, own)
        qfull[s, :, c * CHUNK + LANES : (c + 1) * CHUNK] = jnp.where(upper, own, other)

    for t in range(chunks + bits):
        if t < chunks:
            forward(t)
        for s in range(bits):
            c = t - 1 - s
            if 0 <= c < chunks:
                step(s, c)
    for c in range(chunks):
        for s in range(1, bits):
            finish(s, c)
    for s in range(bits):
        qg_ref[s * rank : (s + 1) * rank] = qfull[s]
    for copy in sent:
        copy.wait_send()


def tree(bits, right_side, leaf_inverse, vt, ut, cores):
    rows_dev, cols = right_side.shape
    lf = leaf_inverse.shape[1]
    levels, rank = vt.shape[:2]
    blocks = rows_dev // lf
    chunks = cols // CHUNK
    local_levels = list(range(bits, levels))
    assert blocks == 2 ** len(local_levels) and bits >= 2
    gram_cols = pl.cdiv(rank * (bits - 1), LANES) * LANES
    out_shape = [jax.ShapeDtypeStruct((rank * bits, cols), F32)]
    if local_levels:
        out_shape.append(jax.ShapeDtypeStruct((rank * (2 * blocks - 2), cols), F32))
    vmem = pl.BlockSpec(memory_space=pltpu.VMEM)
    hbm = pl.BlockSpec(memory_space=pl.ANY)
    counts = [2 ** (level - bits) for level in local_levels]
    rest = rank * (bits - 1)
    scratch = [
        pltpu.VMEM((chunks, rows_dev, CHUNK), F32),
        pltpu.VMEM((rows_dev, lf), F32),
        pltpu.VMEM((bits, 2 * rank, 2 * rank), F32),
        pltpu.VMEM((blocks, levels * rank, lf), F32),
        pltpu.SemaphoreType.DMA((1 + levels + chunks,)),
        pltpu.VMEM((bits - 1, rest, gram_cols), F32),
        pltpu.VMEM((bits - 1, rest, gram_cols), F32),
        pltpu.VMEM((chunks, 2 * rank + rest, LANES), F32),
        pltpu.VMEM((chunks, 2 * rank + rest, LANES), F32),
        pltpu.VMEM((bits, chunks, rest, LANES), F32),
        pltpu.VMEM((bits, chunks, rest, LANES), F32),
        pltpu.VMEM((bits - 1, chunks, rank, LANES), F32),
        pltpu.VMEM((bits - 1, chunks, rank, LANES), F32),
        pltpu.VMEM((bits, rank, cols), F32),
        pltpu.SemaphoreType.DMA((bits - 1, 2)),
        pltpu.SemaphoreType.DMA((chunks, 2)),
        pltpu.SemaphoreType.DMA((bits - 1, chunks, 2)),
        pltpu.SemaphoreType.DMA((bits - 1, chunks, 2)),
    ]
    scratch += [pltpu.VMEM((count, 2 * rank, 2 * rank), F32) for count in counts]
    scratch += [
        pltpu.VMEM((count, rank * (level + 2), 2 * rank), F32)
        for count, level in zip(counts, local_levels)
    ]
    return pl.pallas_call(
        functools.partial(tree_kernel, bits, levels, blocks),
        out_shape=out_shape,
        in_specs=[hbm, hbm, vmem, vmem, hbm],
        out_specs=[vmem] * len(out_shape),
        scratch_shapes=scratch,
        compiler_params=pltpu.CompilerParams(
            collective_id=0, has_side_effects=True, vmem_limit_bytes=56 << 20
        ),
        name="tree",
    )(right_side, leaf_inverse, vt, ut, cores)


def apply_kernel(bits, levels, blocks, right_ref, leaf_ref, ut_ref, qg_ref, *refs):
    ql_ref = refs[0] if levels > bits else None
    out_ref, high_ref, low_ref = refs[-3:]
    rank, rows_dev = ut_ref.shape[1:]
    lf = rows_dev // blocks
    pad = high_ref.shape[1] - lf - levels * rank

    @pl.when(pl.program_id(0) == 0)
    def _():
        high, low = split(leaf_ref[...])
        high_ref[:, :lf] = high
        low_ref[:, :lf] = low
        rows = [ut_ref[level] for level in level_order(bits, levels)]
        if pad:
            rows.append(jnp.zeros((pad, rows_dev), F32))
        high, low = split(-jnp.concatenate(rows, 0).T)
        high_ref[:, lf:] = high
        low_ref[:, lf:] = low

    q_high, q_low = split(qg_ref[...])
    if ql_ref is not None:
        l_high, l_low = split(ql_ref[...])
    zero = [jnp.zeros((pad, out_ref.shape[1]), jnp.bfloat16)] if pad else []
    for i in range(blocks):
        rows = slice(i * lf, (i + 1) * lf)
        x_high, x_low = split(right_ref[rows, :])
        highs, lows = [x_high, q_high], [x_low, q_low]
        for level in range(bits, levels):
            start = local_offset(level, bits, rank) + rank * (i * 2 ** (level - bits + 1) // blocks)
            highs.append(l_high[start : start + rank])
            lows.append(l_low[start : start + rank])
        x_high = jnp.concatenate(highs + zero, 0)
        x_low = jnp.concatenate(lows + zero, 0)
        a_high, a_low = high_ref[rows, :], low_ref[rows, :]
        out_ref[rows, :] = (
            jnp.dot(a_high, x_high, preferred_element_type=F32)
            + jnp.dot(a_high, x_low, preferred_element_type=F32)
            + jnp.dot(a_low, x_high, preferred_element_type=F32)
        )


def apply(bits, right_side, leaf_inverse, ut, qs):
    rows_dev, cols = right_side.shape
    lf = leaf_inverse.shape[1]
    levels, rank = ut.shape[:2]
    blocks = rows_dev // lf
    depth = lf + pl.cdiv(levels * rank, LANES) * LANES
    width = CHUNK

    def column(rows):
        return pl.BlockSpec((rows, width), lambda c: (0, c))

    return pl.pallas_call(
        functools.partial(apply_kernel, bits, levels, blocks),
        grid=(cols // width,),
        out_shape=jax.ShapeDtypeStruct((rows_dev, cols), F32),
        in_specs=[
            column(rows_dev),
            pl.BlockSpec((rows_dev, lf), lambda c: (0, 0)),
            pl.BlockSpec(ut.shape, lambda c: (0, 0, 0)),
        ]
        + [column(q.shape[0]) for q in qs],
        out_specs=column(rows_dev),
        scratch_shapes=[pltpu.VMEM((rows_dev, depth), jnp.bfloat16)] * 2,
        compiler_params=pltpu.CompilerParams(vmem_limit_bytes=56 << 20),
        name="apply",
    )(right_side, leaf_inverse, ut, *qs)


def local(bits, right_side, leaf_inverse, left_factors, right_factors, cores):
    ut = jnp.swapaxes(left_factors, 1, 2)
    vt = jnp.swapaxes(right_factors, 1, 2)
    qs = tree(bits, right_side, leaf_inverse, vt, ut, cores)
    return apply(bits, right_side, leaf_inverse, ut, qs)


def solution(mesh):
    bits = mesh.shape["rows"].bit_length() - 1
    in_specs = (
        P(("rep", "rows"), None),
        P(("rep", "rows"), None),
        P(None, ("rep", "rows"), None),
        P(None, ("rep", "rows"), None),
        P("rep", None, None),
    )
    out_specs = P(("rep", "rows"), None)
    return jax.shard_map(
        functools.partial(local, bits),
        mesh=mesh,
        in_specs=in_specs,
        out_specs=out_specs,
        check_vma=False,
    )
```

```python
import functools

import jax
import jax.numpy as jnp
from jax import lax
from jax.experimental import pallas as pl
from jax.experimental.pallas import tpu as pltpu
from jax.sharding import PartitionSpec as P

LANES = 128
CHUNK = 2 * LANES
HIGH = lax.Precision.HIGH
F32 = jnp.float32
TREE_VMEM = 56 << 20
APPLY_VMEM = 56 << 20


def dot(a, b):
    return jnp.dot(a, b, precision=HIGH, preferred_element_type=F32)


def dot_nt(a, b):
    return lax.dot_general(
        a, b, (((1,), (1,)), ((), ())), precision=HIGH, preferred_element_type=F32
    )


def split(x):
    high = x.astype(jnp.bfloat16)
    return high, (x - high.astype(F32)).astype(jnp.bfloat16)


def level_order(bits, levels):
    return [bits - 1 - s for s in range(bits)] + list(range(bits, levels))


def local_offset(level, bits, rank):
    return rank * (2 ** (level - bits + 1) - 2)


def dot3(a_high, a_low, b_high, b_low):
    def one(a, b):
        return jnp.dot(a, b, preferred_element_type=F32)

    return one(a_high, b_high) + one(a_high, b_low) + one(a_low, b_high)


def tree_kernel(bits, levels, blocks, right_hbm, leaf_hbm, vt_hbm, ut_hbm, cores_hbm, *refs):
    x_hbm, qg_hbm, uh_hbm, ul_hbm = refs[:4]
    rbuf, leaf, vt_ref, ut_ref, core_g, sem_in, sem_out = refs[4:11]
    r_high, r_low, a_high, a_low, m_high, m_low, u_high, u_low, ql_ref, q_first = refs[11:21]
    gram_out, gram_in, first_out, first_in, later_out, later_in, q_out = refs[21:28]
    gram_sem, first_sem, later_sem, q_sem = refs[28:32]
    local_levels = list(range(bits, levels))
    core_l = refs[32 : 32 + len(local_levels)]
    ch_refs = refs[32 + len(local_levels) :]

    me = lax.axis_index("rows")
    rank, rows_dev = vt_ref.shape[1:]
    chunks = rbuf.shape[0]
    lf = rows_dev // blocks
    half_id = lax.rem(me, 2)
    upper = half_id == 1
    order = level_order(bits, levels)

    def child(s):
        return lax.rem(me // 2**s, 2)

    def partner(s):
        return me + (1 - 2 * child(s)) * 2**s

    barrier = pltpu.get_barrier_semaphore()
    for s in range(bits):
        pl.semaphore_signal(
            barrier, inc=1, device_id={"rows": partner(s)}, device_id_type=pl.DeviceIdType.MESH
        )

    slots = {"in": 0, "out": 0}

    def move(src, dst, sems, kind):
        copy = pltpu.make_async_copy(src, dst, sems.at[slots[kind]])
        slots[kind] += 1
        copy.start()
        return copy

    factor_loads = [move(vt_hbm, vt_ref, sem_in, "in"), move(ut_hbm, ut_ref, sem_in, "in")]
    leaf_load = move(leaf_hbm, leaf, sem_in, "in")
    core_loads = []
    for n, level in enumerate(local_levels):
        count = 2 ** (level - bits)
        src = cores_hbm.at[pl.ds(2**level - 1 + me * count, count)]
        core_loads.append(move(src, core_l[n], sem_in, "in"))
    right_loads = [
        move(right_hbm.at[:, pl.ds(c * CHUNK, CHUNK)], rbuf.at[c], sem_in, "in")
        for c in range(chunks)
    ]
    core_g_loads = []
    for s in range(bits):
        src = cores_hbm.at[2 ** (bits - 1 - s) - 1 + me // 2 ** (s + 1)]
        core_g_loads.append(move(src, core_g.at[s], sem_in, "in"))

    sent, written = [], []

    def send(src, dst, sems, s):
        copy = pltpu.make_async_remote_copy(
            src_ref=src,
            dst_ref=dst,
            send_sem=sems.at[0],
            recv_sem=sems.at[1],
            device_id={"rows": partner(s)},
            device_id_type=pl.DeviceIdType.MESH,
        )
        copy.start()
        sent.append(copy)
        return copy

    for copy in factor_loads:
        copy.wait()
    gram_cols = gram_out.shape[2]
    u_rows = [ut_ref[bits - 1 - s] for s in range(bits - 1)]
    pad = gram_cols - rank * (bits - 1)
    if pad:
        u_rows.append(jnp.zeros((pad, rows_dev), F32))
    v_rows = [vt_ref[bits - 1 - s] for s in range(1, bits)]
    gram_out[0] = dot_nt(jnp.concatenate(v_rows, 0), jnp.concatenate(u_rows, 0))
    pl.semaphore_wait(barrier, bits)
    gram_copy = {0: send(gram_out.at[0], gram_in.at[0], gram_sem.at[0], 0)}

    vt_all = jnp.concatenate([vt_ref[level] for level in order], 0)
    for copy in core_loads:
        copy.wait()
    for n, level in enumerate(local_levels):
        count = 2 ** (level - bits)
        node = rows_dev // count
        half = node // 2
        zero = jnp.zeros((rank, half), F32)
        for k in range(count):
            base = k * node
            u_a = ut_ref[level, :, base : base + half]
            u_b = ut_ref[level, :, base + half : base + node]
            diag = jnp.concatenate(
                [jnp.concatenate([u_a, zero], 1), jnp.concatenate([zero, u_b], 1)], 0
            )
            gram = dot_nt(vt_all[: rank * level, base : base + node], diag)
            core = core_l[n][k]
            ch_refs[n][k, : 2 * rank] = core
            ch_refs[n][k, 2 * rank :] = dot(gram, core)
    leaf_load.wait()
    high, low = split(leaf[...])
    a_high[:, :lf] = high
    a_low[:, :lf] = low
    v_high, v_low = split(vt_all)
    for i in range(blocks):
        rows = slice(i * lf, (i + 1) * lf)
        high, low = split(
            dot3(v_high[:, rows], v_low[:, rows], a_high[rows, :lf], a_low[rows, :lf])
        )
        m_high[i] = high
        m_low[i] = low

    first_copy, later_copy, q_copy = {}, {}, {}

    def forward(c):
        right_loads[c].wait()
        high, low = split(rbuf[c])
        r_high[c] = high
        r_low[c] = low
        parts = []
        for i in range(blocks):
            rows = slice(i * lf, (i + 1) * lf)
            parts.append(dot3(m_high[i], m_low[i], r_high[c, rows, :], r_low[c, rows, :]))
        for n in reversed(range(len(local_levels))):
            level = local_levels[n]
            top = rank * level
            merged = []
            for k in range(len(parts) // 2):
                a, b = parts[2 * k], parts[2 * k + 1]
                image = dot(ch_refs[n][k], jnp.concatenate([b[top:], a[top:]], 0))
                start = local_offset(level, bits, rank) + 2 * rank * k
                ql_ref[c, start : start + 2 * rank] = image[: 2 * rank]
                merged.append(a[:top] + b[:top] - image[2 * rank :])
            parts = merged
        p = parts[0]
        low, high = p[:, :LANES], p[:, LANES:]
        first_out[c, :rank] = low[:rank]
        first_out[c, rank : 2 * rank] = high[:rank]
        first_out[c, 2 * rank :] = jnp.where(upper, low[rank:], high[rank:])
        first_copy[c] = send(first_out.at[c], first_in.at[c], first_sem.at[c], 0)
        later_out[0, c] = jnp.where(upper, high[rank:], low[rank:])

    def bases():
        if local_levels:
            rows = [ut_ref[level] for level in local_levels]
            extra = a_high.shape[1] - lf - rank * len(rows)
            if extra:
                rows.append(jnp.zeros((extra, rows_dev), F32))
            high, low = split(-jnp.concatenate(rows, 0).T)
            a_high[:, lf:] = high
            a_low[:, lf:] = low
        rows = [ut_ref[bits - 1 - s] for s in range(bits)]
        extra = u_high.shape[1] - rank * bits
        if extra:
            rows.append(jnp.zeros((extra, rows_dev), F32))
        high, low = split(-jnp.concatenate(rows, 0).T)
        u_high[...] = high
        u_low[...] = low
        written.append(move(u_high, uh_hbm, sem_out, "out"))
        written.append(move(u_low, ul_hbm, sem_out, "out"))

    def leaves(c):
        for i in range(blocks):
            rows = slice(i * lf, (i + 1) * lf)
            highs, lows = [r_high[c, rows, :]], [r_low[c, rows, :]]
            width = lf
            for level in local_levels:
                place = rank * (i * 2 ** (level - bits + 1) // blocks)
                start = local_offset(level, bits, rank) + place
                high, low = split(ql_ref[c, start : start + rank])
                highs.append(high)
                lows.append(low)
                width += rank
            if a_high.shape[1] > width:
                zero = jnp.zeros((a_high.shape[1] - width, CHUNK), jnp.bfloat16)
                highs.append(zero)
                lows.append(zero)
            rbuf[c, rows, :] = dot3(
                a_high[rows, :],
                a_low[rows, :],
                jnp.concatenate(highs, 0),
                jnp.concatenate(lows, 0),
            )
        written.append(move(rbuf.at[c], x_hbm.at[:, pl.ds(c * CHUNK, CHUNK)], sem_out, "out"))

    def stack(mine, theirs, s):
        first = child(s) == 0
        return jnp.concatenate([jnp.where(first, theirs, mine), jnp.where(first, mine, theirs)], 0)

    def pick(image, s):
        first = child(s) == 0
        return (
            jnp.where(first, image[:rank], image[rank:]),
            jnp.where(first, image[rank:], image[:rank]),
        )

    def correction(s, own, sib):
        zeros = [jnp.zeros((rank, LANES), F32)]
        before, after = s, gram_cols // rank - 1 - s
        rows = slice(rank * s, None)
        q_own = jnp.concatenate(zeros * before + [own] + zeros * after, 0)
        q_sib = jnp.concatenate(zeros * before + [sib] + zeros * after, 0)
        return dot(gram_out[s, rows, :], q_own) + dot(gram_in[s, rows, :], q_sib)

    def grams(s):
        gram_copy[s].wait_recv()
        if s + 1 < bits - 1:
            gram_out[s + 1] = gram_out[s] + gram_in[s]
            gram_copy[s + 1] = send(
                gram_out.at[s + 1], gram_in.at[s + 1], gram_sem.at[s + 1], s + 1
            )

    def step(s, c):
        if c == 0:
            core_g_loads[s].wait()
        if s == 0:
            first_copy[c].wait_recv()
            mine = jnp.concatenate([first_out[c, :rank], first_out[c, rank : 2 * rank]], 1)
            theirs = jnp.concatenate([first_in[c, :rank], first_in[c, rank : 2 * rank]], 1)
            image = dot(core_g[0], stack(mine, theirs, 0))
            own, sib = pick(image, 0)
            q_first[c] = own
            own = jnp.where(upper, own[:, LANES:], own[:, :LANES])
            sib = jnp.where(upper, sib[:, LANES:], sib[:, :LANES])
            rest = later_out[0, c] + first_in[c, 2 * rank :]
        else:
            later_copy[s, c].wait_recv()
            live = slice(rank * (s - 1), rank * s)
            image = dot(core_g[s], stack(later_out[s, c, live], later_in[s, c, live], s))
            own, sib = pick(image, s)
            q_out[s - 1, c] = own
            start = pl.multiple_of(c * CHUNK + half_id * LANES, LANES)
            target = qg_hbm.at[pl.ds(s * rank, rank), pl.ds(start, LANES)]
            q_copy[s, c] = send(q_out.at[s - 1, c], target, q_sem.at[s - 1, c], 0)
            if s < bits - 1:
                rest = later_out[s, c, rank * s :] + later_in[s, c, rank * s :]
        if s < bits - 1:
            later_out[s + 1, c, rank * s :] = rest - correction(s, own, sib)
            later_copy[s + 1, c] = send(
                later_out.at[s + 1, c, pl.ds(rank * s, rank * (bits - 1 - s))],
                later_in.at[s + 1, c, pl.ds(rank * s, rank * (bits - 1 - s))],
                later_sem.at[s, c],
                s + 1,
            )
        if s == 0:
            target = qg_hbm.at[pl.ds(0, rank), pl.ds(c * CHUNK, CHUNK)]
            written.append(move(q_first.at[c], target, sem_out, "out"))
        else:
            written.append(move(q_out.at[s - 1, c], target, sem_out, "out"))

    for c in range(chunks):
        forward(c)
        if c == 0:
            grams(0)
    for s in range(1, bits - 1):
        grams(s)
    bases()
    for t in range(chunks + bits - 1):
        for s in range(bits):
            c = t - s
            if 0 <= c < chunks:
                step(s, c)
        if t < chunks:
            leaves(t)
    for copy in q_copy.values():
        copy.wait_recv()
    for copy in written:
        copy.wait()
    for copy in sent:
        copy.wait_send()


def tree(bits, right_side, leaf_inverse, vt, ut, cores):
    rows_dev, cols = right_side.shape
    lf = leaf_inverse.shape[1]
    levels, rank = vt.shape[:2]
    blocks = rows_dev // lf
    chunks = cols // CHUNK
    local_levels = list(range(bits, levels))
    assert blocks == 2 ** len(local_levels) and bits >= 2
    gram_cols = pl.cdiv(rank * (bits - 1), LANES) * LANES
    depth = lf + pl.cdiv(rank * len(local_levels), LANES) * LANES
    wide = pl.cdiv(rank * bits, LANES) * LANES
    out_shape = [
        jax.ShapeDtypeStruct((rows_dev, cols), F32),
        jax.ShapeDtypeStruct((rank * bits, cols), F32),
        jax.ShapeDtypeStruct((rows_dev, wide), jnp.bfloat16),
        jax.ShapeDtypeStruct((rows_dev, wide), jnp.bfloat16),
    ]
    hbm = pl.BlockSpec(memory_space=pl.ANY)
    counts = [2 ** (level - bits) for level in local_levels]
    rest = rank * (bits - 1)
    half = jnp.bfloat16
    scratch = [
        pltpu.VMEM((chunks, rows_dev, CHUNK), F32),
        pltpu.VMEM((rows_dev, lf), F32),
        pltpu.VMEM((levels, rank, rows_dev), F32),
        pltpu.VMEM((levels, rank, rows_dev), F32),
        pltpu.VMEM((bits, 2 * rank, 2 * rank), F32),
        pltpu.SemaphoreType.DMA((3 + levels + chunks,)),
        pltpu.SemaphoreType.DMA((2 + chunks * (bits + 1),)),
        pltpu.VMEM((chunks, rows_dev, CHUNK), half),
        pltpu.VMEM((chunks, rows_dev, CHUNK), half),
        pltpu.VMEM((rows_dev, depth), half),
        pltpu.VMEM((rows_dev, depth), half),
        pltpu.VMEM((blocks, levels * rank, lf), half),
        pltpu.VMEM((blocks, levels * rank, lf), half),
        pltpu.VMEM((rows_dev, wide), half),
        pltpu.VMEM((rows_dev, wide), half),
        pltpu.VMEM((chunks, max(rank * (2 * blocks - 2), rank), CHUNK), F32),
        pltpu.VMEM((chunks, rank, CHUNK), F32),
        pltpu.VMEM((bits - 1, rest, gram_cols), F32),
        pltpu.VMEM((bits - 1, rest, gram_cols), F32),
        pltpu.VMEM((chunks, 2 * rank + rest, LANES), F32),
        pltpu.VMEM((chunks, 2 * rank + rest, LANES), F32),
        pltpu.VMEM((bits, chunks, rest, LANES), F32),
        pltpu.VMEM((bits, chunks, rest, LANES), F32),
        pltpu.VMEM((bits - 1, chunks, rank, LANES), F32),
        pltpu.SemaphoreType.DMA((bits - 1, 2)),
        pltpu.SemaphoreType.DMA((chunks, 2)),
        pltpu.SemaphoreType.DMA((bits - 1, chunks, 2)),
        pltpu.SemaphoreType.DMA((bits - 1, chunks, 2)),
    ]
    scratch += [pltpu.VMEM((count, 2 * rank, 2 * rank), F32) for count in counts]
    scratch += [
        pltpu.VMEM((count, rank * (level + 2), 2 * rank), F32)
        for count, level in zip(counts, local_levels)
    ]
    return pl.pallas_call(
        functools.partial(tree_kernel, bits, levels, blocks),
        out_shape=out_shape,
        in_specs=[hbm] * 5,
        out_specs=[hbm] * 4,
        scratch_shapes=scratch,
        compiler_params=pltpu.CompilerParams(
            collective_id=0, has_side_effects=True, vmem_limit_bytes=TREE_VMEM
        ),
        name="tree",
    )(right_side, leaf_inverse, vt, ut, cores)


def apply_kernel(x_ref, uh_ref, ul_ref, q_ref, out_ref):
    pad = uh_ref.shape[1] - q_ref.shape[0]
    q = q_ref[...]
    if pad:
        q = jnp.concatenate([q, jnp.zeros((pad, q.shape[1]), F32)], 0)
    high, low = split(q)
    out_ref[...] = x_ref[...] + dot3(uh_ref[...], ul_ref[...], high, low)


def apply(x, q, u_high, u_low):
    rows_dev, cols = x.shape
    width = CHUNK

    def column(rows):
        return pl.BlockSpec((rows, width), lambda c: (0, c))

    whole = pl.BlockSpec(u_high.shape, lambda c: (0, 0))
    return pl.pallas_call(
        apply_kernel,
        grid=(cols // width,),
        out_shape=jax.ShapeDtypeStruct((rows_dev, cols), F32),
        in_specs=[column(rows_dev), whole, whole, column(q.shape[0])],
        out_specs=column(rows_dev),
        compiler_params=pltpu.CompilerParams(vmem_limit_bytes=APPLY_VMEM),
        name="apply",
    )(x, u_high, u_low, q)


def local(bits, right_side, leaf_inverse, left_factors, right_factors, cores):
    ut = jnp.swapaxes(left_factors, 1, 2)
    vt = jnp.swapaxes(right_factors, 1, 2)
    x, q, u_high, u_low = tree(bits, right_side, leaf_inverse, vt, ut, cores)
    return apply(x, q, u_high, u_low)


def solution(mesh):
    bits = mesh.shape["rows"].bit_length() - 1
    in_specs = (
        P(("rep", "rows"), None),
        P(("rep", "rows"), None),
        P(None, ("rep", "rows"), None),
        P(None, ("rep", "rows"), None),
        P("rep", None, None),
    )
    out_specs = P(("rep", "rows"), None)
    return jax.shard_map(
        functools.partial(local, bits),
        mesh=mesh,
        in_specs=in_specs,
        out_specs=out_specs,
        check_vma=False,
    )
```

```python
import functools

import jax
import jax.numpy as jnp
from jax import lax
from jax.experimental import pallas as pl
from jax.experimental.pallas import tpu as pltpu
from jax.sharding import PartitionSpec as P

LANES = 128
CHUNK = 2 * LANES
F32 = jnp.float32
TREE_VMEM = 24 << 20
APPLY_VMEM = 12 << 20


def split(x):
    high = x.astype(jnp.bfloat16)
    return high, (x - high.astype(F32)).astype(jnp.bfloat16)


def level_order(bits, levels):
    return [bits - 1 - s for s in range(bits)] + list(range(bits, levels))


def local_offset(level, bits, rank):
    return rank * (2 ** (level - bits + 1) - 2)


def dot3(a, b, nt=False):
    dims = (((1,), (1 if nt else 0,)), ((), ()))

    def one(x, y):
        return lax.dot_general(x, y, dims, preferred_element_type=F32)

    return one(a[0], b[0]) + one(a[0], b[1]) + one(a[1], b[0])


def dot(a, b):
    return dot3(split(a), split(b))


def tree_kernel(bits, levels, blocks, right_hbm, leaf_hbm, vt_hbm, ut_hbm, cores_hbm, *refs):
    x_hbm, qg_hbm, uh_hbm, ul_hbm = refs[:4]
    rbuf, leaf, vt_ref, ut_ref, core_g, sem_in, sem_out = refs[4:11]
    r_high, r_low, a_high, a_low, m_high, m_low, u_high, u_low, ql_ref, q_first = refs[11:21]
    gram_out, gram_in, first_out, first_in, later_out, later_in, q_out = refs[21:28]
    gram_sem, first_sem, later_sem, q_sem = refs[28:32]
    local_levels = list(range(bits, levels))
    core_l = refs[32 : 32 + len(local_levels)]
    ch_refs = refs[32 + len(local_levels) :]
    ch_refs = list(zip(ch_refs[::2], ch_refs[1::2]))

    me = lax.axis_index("rows")
    rank, rows_dev = vt_ref.shape[1:]
    chunks = rbuf.shape[0]
    lf = rows_dev // blocks
    half_id = lax.rem(me, 2)
    upper = half_id == 1
    order = level_order(bits, levels)

    def child(s):
        return lax.rem(me // 2**s, 2)

    def partner(s):
        return me + (1 - 2 * child(s)) * 2**s

    barrier = pltpu.get_barrier_semaphore()
    for s in range(bits):
        pl.semaphore_signal(
            barrier, inc=1, device_id={"rows": partner(s)}, device_id_type=pl.DeviceIdType.MESH
        )

    slots = {"in": 0, "out": 0}

    def move(src, dst, sems, kind):
        copy = pltpu.make_async_copy(src, dst, sems.at[slots[kind]])
        slots[kind] += 1
        copy.start()
        return copy

    factor_loads = [move(vt_hbm, vt_ref, sem_in, "in"), move(ut_hbm, ut_ref, sem_in, "in")]
    leaf_load = move(leaf_hbm, leaf, sem_in, "in")
    core_loads = []
    for n, level in enumerate(local_levels):
        count = 2 ** (level - bits)
        src = cores_hbm.at[pl.ds(2**level - 1 + me * count, count)]
        core_loads.append(move(src, core_l[n], sem_in, "in"))
    right_loads = [
        move(right_hbm.at[:, pl.ds(c * CHUNK, CHUNK)], rbuf.at[c], sem_in, "in")
        for c in range(chunks)
    ]
    core_g_loads = []
    for s in range(bits):
        src = cores_hbm.at[2 ** (bits - 1 - s) - 1 + me // 2 ** (s + 1)]
        core_g_loads.append(move(src, core_g.at[s], sem_in, "in"))

    sent, written = [], []

    def send(src, dst, sems, s):
        copy = pltpu.make_async_remote_copy(
            src_ref=src,
            dst_ref=dst,
            send_sem=sems.at[0],
            recv_sem=sems.at[1],
            device_id={"rows": partner(s)},
            device_id_type=pl.DeviceIdType.MESH,
        )
        copy.start()
        sent.append(copy)
        return copy

    for copy in factor_loads:
        copy.wait()
    gram_cols = gram_out.shape[2]
    vt = split(jnp.concatenate([vt_ref[level] for level in order], 0))
    ut = split(jnp.concatenate([ut_ref[level] for level in order], 0))
    v_rows = [v[rank : rank * bits] for v in vt]
    u_rows = [u[:gram_cols] for u in ut]
    gram_out[0] = dot3(v_rows, u_rows, nt=True)
    pl.semaphore_wait(barrier, bits)
    gram_copy = {0: send(gram_out.at[0], gram_in.at[0], gram_sem.at[0], 0)}

    for copy in core_loads:
        copy.wait()
    for n, level in enumerate(local_levels):
        count = 2 ** (level - bits)
        node = rows_dev // count
        half = node // 2
        zero = jnp.zeros((rank, half), jnp.bfloat16)
        own = slice(rank * level, rank * (level + 1))
        for k in range(count):
            base = k * node
            diag = [
                jnp.concatenate(
                    [
                        jnp.concatenate([u[own, base : base + half], zero], 1),
                        jnp.concatenate([zero, u[own, base + half : base + node]], 1),
                    ],
                    0,
                )
                for u in ut
            ]
            gram = dot3([v[: rank * level, base : base + node] for v in vt], diag, nt=True)
            core = core_l[n][k]
            for ref, top, rest in zip(ch_refs[n], split(core), split(dot(gram, core))):
                ref[k, : 2 * rank] = top
                ref[k, 2 * rank :] = rest
    leaf_load.wait()
    high, low = split(leaf[...])
    a_high[:, :lf] = high
    a_low[:, :lf] = low
    for i in range(blocks):
        rows = slice(i * lf, (i + 1) * lf)
        high, low = split(
            dot3([v[:, rows] for v in vt], (a_high[rows, :lf], a_low[rows, :lf]))
        )
        m_high[i] = high
        m_low[i] = low

    first_copy, later_copy, q_copy = {}, {}, {}

    def forward(c):
        right_loads[c].wait()
        high, low = split(rbuf[c])
        r_high[c] = high
        r_low[c] = low
        parts = []
        for i in range(blocks):
            rows = slice(i * lf, (i + 1) * lf)
            parts.append(dot3((m_high[i], m_low[i]), (r_high[c, rows, :], r_low[c, rows, :])))
        for n in reversed(range(len(local_levels))):
            level = local_levels[n]
            top = rank * level
            merged = []
            for k in range(len(parts) // 2):
                a, b = parts[2 * k], parts[2 * k + 1]
                both = jnp.concatenate([b[top:], a[top:]], 0)
                image = dot3((ch_refs[n][0][k], ch_refs[n][1][k]), split(both))
                start = local_offset(level, bits, rank) + 2 * rank * k
                ql_ref[c, start : start + 2 * rank] = image[: 2 * rank]
                merged.append(a[:top] + b[:top] - image[2 * rank :])
            parts = merged
        p = parts[0]
        low, high = p[:, :LANES], p[:, LANES:]
        first_out[c, :rank] = low[:rank]
        first_out[c, rank : 2 * rank] = high[:rank]
        first_out[c, 2 * rank :] = jnp.where(upper, low[rank:], high[rank:])
        first_copy[c] = send(first_out.at[c], first_in.at[c], first_sem.at[c], 0)
        later_out[0, c] = jnp.where(upper, high[rank:], low[rank:])

    def bases():
        if local_levels:
            rows = [ut_ref[level] for level in local_levels]
            extra = a_high.shape[1] - lf - rank * len(rows)
            if extra:
                rows.append(jnp.zeros((extra, rows_dev), F32))
            high, low = split(-jnp.concatenate(rows, 0).T)
            a_high[:, lf:] = high
            a_low[:, lf:] = low
        rows = [ut_ref[bits - 1 - s] for s in range(bits)]
        extra = u_high.shape[1] - rank * bits
        if extra:
            rows.append(jnp.zeros((extra, rows_dev), F32))
        high, low = split(-jnp.concatenate(rows, 0).T)
        u_high[...] = high
        u_low[...] = low
        written.append(move(u_high, uh_hbm, sem_out, "out"))
        written.append(move(u_low, ul_hbm, sem_out, "out"))

    def leaves(c):
        for i in range(blocks):
            rows = slice(i * lf, (i + 1) * lf)
            highs, lows = [r_high[c, rows, :]], [r_low[c, rows, :]]
            width = lf
            for level in local_levels:
                place = rank * (i * 2 ** (level - bits + 1) // blocks)
                start = local_offset(level, bits, rank) + place
                high, low = split(ql_ref[c, start : start + rank])
                highs.append(high)
                lows.append(low)
                width += rank
            if a_high.shape[1] > width:
                zero = jnp.zeros((a_high.shape[1] - width, CHUNK), jnp.bfloat16)
                highs.append(zero)
                lows.append(zero)
            rbuf[c, rows, :] = dot3(
                (a_high[rows, :], a_low[rows, :]),
                (jnp.concatenate(highs, 0), jnp.concatenate(lows, 0)),
            )
        written.append(move(rbuf.at[c], x_hbm.at[:, pl.ds(c * CHUNK, CHUNK)], sem_out, "out"))

    def stack(mine, theirs, s):
        first = child(s) == 0
        return jnp.concatenate([jnp.where(first, theirs, mine), jnp.where(first, mine, theirs)], 0)

    def pick(image, s):
        first = child(s) == 0
        return (
            jnp.where(first, image[:rank], image[rank:]),
            jnp.where(first, image[rank:], image[:rank]),
        )

    def correction(s, own, sib):
        zeros = [jnp.zeros((rank, LANES), F32)]
        before, after = s, gram_cols // rank - 1 - s
        rows = slice(rank * s, None)
        q_own = jnp.concatenate(zeros * before + [own] + zeros * after, 0)
        q_sib = jnp.concatenate(zeros * before + [sib] + zeros * after, 0)
        return dot(gram_out[s, rows, :], q_own) + dot(gram_in[s, rows, :], q_sib)

    def grams(s):
        gram_copy[s].wait_recv()
        if s + 1 < bits - 1:
            gram_out[s + 1] = gram_out[s] + gram_in[s]
            gram_copy[s + 1] = send(
                gram_out.at[s + 1], gram_in.at[s + 1], gram_sem.at[s + 1], s + 1
            )

    def step(s, c):
        if c == 0:
            core_g_loads[s].wait()
        if s == 0:
            first_copy[c].wait_recv()
            mine = jnp.concatenate([first_out[c, :rank], first_out[c, rank : 2 * rank]], 1)
            theirs = jnp.concatenate([first_in[c, :rank], first_in[c, rank : 2 * rank]], 1)
            image = dot(core_g[0], stack(mine, theirs, 0))
            own, sib = pick(image, 0)
            q_first[c] = own
            own = jnp.where(upper, own[:, LANES:], own[:, :LANES])
            sib = jnp.where(upper, sib[:, LANES:], sib[:, :LANES])
            rest = later_out[0, c] + first_in[c, 2 * rank :]
        else:
            later_copy[s, c].wait_recv()
            live = slice(rank * (s - 1), rank * s)
            image = dot(core_g[s], stack(later_out[s, c, live], later_in[s, c, live], s))
            own, sib = pick(image, s)
            q_out[s - 1, c] = own
            start = pl.multiple_of(c * CHUNK + half_id * LANES, LANES)
            target = qg_hbm.at[pl.ds(s * rank, rank), pl.ds(start, LANES)]
            q_copy[s, c] = send(q_out.at[s - 1, c], target, q_sem.at[s - 1, c], 0)
            if s < bits - 1:
                rest = later_out[s, c, rank * s :] + later_in[s, c, rank * s :]
        if s < bits - 1:
            later_out[s + 1, c, rank * s :] = rest - correction(s, own, sib)
            later_copy[s + 1, c] = send(
                later_out.at[s + 1, c, pl.ds(rank * s, rank * (bits - 1 - s))],
                later_in.at[s + 1, c, pl.ds(rank * s, rank * (bits - 1 - s))],
                later_sem.at[s, c],
                s + 1,
            )
        if s == 0:
            target = qg_hbm.at[pl.ds(0, rank), pl.ds(c * CHUNK, CHUNK)]
            written.append(move(q_first.at[c], target, sem_out, "out"))
        else:
            written.append(move(q_out.at[s - 1, c], target, sem_out, "out"))

    for c in range(chunks):
        forward(c)
        if c == 0:
            grams(0)
    for s in range(1, bits - 1):
        grams(s)
    bases()
    for t in range(chunks + bits - 1):
        for s in range(bits):
            c = t - s
            if 0 <= c < chunks:
                step(s, c)
        if t < chunks:
            leaves(t)
    for copy in q_copy.values():
        copy.wait_recv()
    for copy in written:
        copy.wait()
    for copy in sent:
        copy.wait_send()


def tree(bits, right_side, leaf_inverse, vt, ut, cores):
    rows_dev, cols = right_side.shape
    lf = leaf_inverse.shape[1]
    levels, rank = vt.shape[:2]
    blocks = rows_dev // lf
    chunks = cols // CHUNK
    local_levels = list(range(bits, levels))
    assert blocks == 2 ** len(local_levels) and bits >= 2
    gram_cols = pl.cdiv(rank * (bits - 1), LANES) * LANES
    depth = lf + pl.cdiv(rank * len(local_levels), LANES) * LANES
    wide = pl.cdiv(rank * bits, LANES) * LANES
    out_shape = [
        jax.ShapeDtypeStruct((rows_dev, cols), F32),
        jax.ShapeDtypeStruct((rank * bits, cols), F32),
        jax.ShapeDtypeStruct((rows_dev, wide), jnp.bfloat16),
        jax.ShapeDtypeStruct((rows_dev, wide), jnp.bfloat16),
    ]
    hbm = pl.BlockSpec(memory_space=pltpu.HBM)
    free = pl.BlockSpec(memory_space=pl.ANY)
    counts = [2 ** (level - bits) for level in local_levels]
    rest = rank * (bits - 1)
    half = jnp.bfloat16
    scratch = [
        pltpu.VMEM((chunks, rows_dev, CHUNK), F32),
        pltpu.VMEM((rows_dev, lf), F32),
        pltpu.VMEM((levels, rank, rows_dev), F32),
        pltpu.VMEM((levels, rank, rows_dev), F32),
        pltpu.VMEM((bits, 2 * rank, 2 * rank), F32),
        pltpu.SemaphoreType.DMA((3 + levels + chunks,)),
        pltpu.SemaphoreType.DMA((2 + chunks * (bits + 1),)),
        pltpu.VMEM((chunks, rows_dev, CHUNK), half),
        pltpu.VMEM((chunks, rows_dev, CHUNK), half),
        pltpu.VMEM((rows_dev, depth), half),
        pltpu.VMEM((rows_dev, depth), half),
        pltpu.VMEM((blocks, levels * rank, lf), half),
        pltpu.VMEM((blocks, levels * rank, lf), half),
        pltpu.VMEM((rows_dev, wide), half),
        pltpu.VMEM((rows_dev, wide), half),
        pltpu.VMEM((chunks, max(rank * (2 * blocks - 2), rank), CHUNK), F32),
        pltpu.VMEM((chunks, rank, CHUNK), F32),
        pltpu.VMEM((bits - 1, rest, gram_cols), F32),
        pltpu.VMEM((bits - 1, rest, gram_cols), F32),
        pltpu.VMEM((chunks, 2 * rank + rest, LANES), F32),
        pltpu.VMEM((chunks, 2 * rank + rest, LANES), F32),
        pltpu.VMEM((bits, chunks, rest, LANES), F32),
        pltpu.VMEM((bits, chunks, rest, LANES), F32),
        pltpu.VMEM((bits - 1, chunks, rank, LANES), F32),
        pltpu.SemaphoreType.DMA((bits - 1, 2)),
        pltpu.SemaphoreType.DMA((chunks, 2)),
        pltpu.SemaphoreType.DMA((bits - 1, chunks, 2)),
        pltpu.SemaphoreType.DMA((bits - 1, chunks, 2)),
    ]
    scratch += [pltpu.VMEM((count, 2 * rank, 2 * rank), F32) for count in counts]
    scratch += [
        pltpu.VMEM((count, rank * (level + 2), 2 * rank), half)
        for count, level in zip(counts, local_levels)
        for _ in range(2)
    ]
    return pl.pallas_call(
        functools.partial(tree_kernel, bits, levels, blocks),
        out_shape=out_shape,
        in_specs=[hbm] * 5,
        out_specs=[free] * 4,
        scratch_shapes=scratch,
        compiler_params=pltpu.CompilerParams(
            collective_id=0, has_side_effects=True, vmem_limit_bytes=TREE_VMEM + 32 * rows_dev * lf
        ),
        name="tree",
    )(right_side, leaf_inverse, vt, ut, cores)


def apply_kernel(x_ref, uh_ref, ul_ref, q_ref, out_ref):
    pad = uh_ref.shape[1] - q_ref.shape[0]
    q = q_ref[...]
    if pad:
        q = jnp.concatenate([q, jnp.zeros((pad, q.shape[1]), F32)], 0)
    high, low = split(q)
    out_ref[...] = x_ref[...] + dot3((uh_ref[...], ul_ref[...]), (high, low))


def apply(x, q, u_high, u_low):
    rows_dev, cols = x.shape
    width = CHUNK

    def column(rows):
        return pl.BlockSpec((rows, width), lambda c: (0, c))

    whole = pl.BlockSpec(u_high.shape, lambda c: (0, 0))
    return pl.pallas_call(
        apply_kernel,
        grid=(cols // width,),
        out_shape=jax.ShapeDtypeStruct((rows_dev, cols), F32),
        in_specs=[column(rows_dev), whole, whole, column(q.shape[0])],
        out_specs=column(rows_dev),
        compiler_params=pltpu.CompilerParams(vmem_limit_bytes=APPLY_VMEM),
        name="apply",
    )(x, u_high, u_low, q)


def local(bits, right_side, leaf_inverse, left_factors, right_factors, cores):
    ut = jnp.swapaxes(left_factors, 1, 2)
    vt = jnp.swapaxes(right_factors, 1, 2)
    right_side, leaf_inverse, vt, ut, cores = (
        pltpu.with_memory_space_constraint(a, pltpu.HBM)
        for a in (right_side, leaf_inverse, vt, ut, cores)
    )
    x, q, u_high, u_low = tree(bits, right_side, leaf_inverse, vt, ut, cores)
    return apply(x, q, u_high, u_low)


def solution(mesh):
    bits = mesh.shape["rows"].bit_length() - 1
    in_specs = (
        P(("rep", "rows"), None),
        P(("rep", "rows"), None),
        P(None, ("rep", "rows"), None),
        P(None, ("rep", "rows"), None),
        P("rep", None, None),
    )
    out_specs = P(("rep", "rows"), None)
    return jax.shard_map(
        functools.partial(local, bits),
        mesh=mesh,
        in_specs=in_specs,
        out_specs=out_specs,
        check_vma=False,
    )
```

```python
import functools

import jax
import jax.numpy as jnp
from jax import lax
from jax.experimental import pallas as pl
from jax.experimental.pallas import tpu as pltpu
from jax.sharding import PartitionSpec as P

LANES = 128
CHUNK = 2 * LANES
F32 = jnp.float32
TREE_VMEM = 24 << 20
APPLY_VMEM = 12 << 20


def split(x):
    high = x.astype(jnp.bfloat16)
    return high, (x - high.astype(F32)).astype(jnp.bfloat16)


def level_order(bits, levels):
    return [bits - 1 - s for s in range(bits)] + list(range(bits, levels))


def local_offset(level, bits, rank):
    return rank * (2 ** (level - bits + 1) - 2)


def dot3(a, b, nt=False):
    dims = (((1,), (1 if nt else 0,)), ((), ()))

    def one(x, y):
        return lax.dot_general(x, y, dims, preferred_element_type=F32)

    return one(a[0], b[0]) + one(a[0], b[1]) + one(a[1], b[0])


def dot(a, b):
    return dot3(split(a), split(b))


def tree_kernel(bits, levels, blocks, right_hbm, leaf_hbm, vt_hbm, ut_hbm, cores_hbm, *refs):
    x_hbm, qg_hbm, uh_hbm, ul_hbm = refs[:4]
    rbuf, leaf, vt_ref, ut_ref, core_g, sem_in, sem_out = refs[4:11]
    r_high, r_low, a_high, a_low, m_high, m_low, u_high, u_low, ql_ref, q_first = refs[11:21]
    gram_out, gram_in, first_out, first_in, later_out, later_in, q_out = refs[21:28]
    gram_sem, first_sem, later_sem, q_sem = refs[28:32]
    last_in, last_q, last_sem = refs[32:35]
    local_levels = list(range(bits, levels))
    core_l = refs[35 : 35 + len(local_levels)]
    ch_refs = refs[35 + len(local_levels) :]
    ch_refs = list(zip(ch_refs[::2], ch_refs[1::2]))

    me = lax.axis_index("rows")
    rank, rows_dev = vt_ref.shape[1:]
    chunks = rbuf.shape[0]
    lf = rows_dev // blocks
    half_id = lax.rem(me, 2)
    upper = half_id == 1
    order = level_order(bits, levels)

    def child(s):
        return lax.rem(me // 2**s, 2)

    def partner(s):
        return me + (1 - 2 * child(s)) * 2**s

    cross = partner(bits - 1) + (1 - 2 * child(0))
    barrier = pltpu.get_barrier_semaphore()
    for target in [partner(s) for s in range(bits)] + [cross]:
        pl.semaphore_signal(
            barrier, inc=1, device_id={"rows": target}, device_id_type=pl.DeviceIdType.MESH
        )

    slots = {"in": 0, "out": 0}

    def move(src, dst, sems, kind):
        copy = pltpu.make_async_copy(src, dst, sems.at[slots[kind]])
        slots[kind] += 1
        copy.start()
        return copy

    factor_loads = [move(vt_hbm, vt_ref, sem_in, "in"), move(ut_hbm, ut_ref, sem_in, "in")]
    leaf_load = move(leaf_hbm, leaf, sem_in, "in")
    core_loads = []
    for n, level in enumerate(local_levels):
        count = 2 ** (level - bits)
        src = cores_hbm.at[pl.ds(2**level - 1 + me * count, count)]
        core_loads.append(move(src, core_l[n], sem_in, "in"))
    right_loads = [
        move(right_hbm.at[:, pl.ds(c * CHUNK, CHUNK)], rbuf.at[c], sem_in, "in")
        for c in range(chunks)
    ]
    core_g_loads = []
    for s in range(bits):
        src = cores_hbm.at[2 ** (bits - 1 - s) - 1 + me // 2 ** (s + 1)]
        core_g_loads.append(move(src, core_g.at[s], sem_in, "in"))

    sent, written = [], []

    def send(src, dst, sems, s, target=None):
        copy = pltpu.make_async_remote_copy(
            src_ref=src,
            dst_ref=dst,
            send_sem=sems.at[0],
            recv_sem=sems.at[1],
            device_id={"rows": partner(s) if target is None else target},
            device_id_type=pl.DeviceIdType.MESH,
        )
        copy.start()
        sent.append(copy)
        return copy

    for copy in factor_loads:
        copy.wait()
    gram_cols = gram_out.shape[2]
    vt = split(jnp.concatenate([vt_ref[level] for level in order], 0))
    ut = split(jnp.concatenate([ut_ref[level] for level in order], 0))
    v_rows = [v[rank : rank * bits] for v in vt]
    u_rows = [u[:gram_cols] for u in ut]
    gram_out[0] = dot3(v_rows, u_rows, nt=True)
    pl.semaphore_wait(barrier, bits + 1)
    gram_copy = {0: send(gram_out.at[0], gram_in.at[0], gram_sem.at[0], 0)}

    for copy in core_loads:
        copy.wait()
    for n, level in enumerate(local_levels):
        count = 2 ** (level - bits)
        node = rows_dev // count
        half = node // 2
        zero = jnp.zeros((rank, half), jnp.bfloat16)
        own = slice(rank * level, rank * (level + 1))
        for k in range(count):
            base = k * node
            diag = [
                jnp.concatenate(
                    [
                        jnp.concatenate([u[own, base : base + half], zero], 1),
                        jnp.concatenate([zero, u[own, base + half : base + node]], 1),
                    ],
                    0,
                )
                for u in ut
            ]
            gram = dot3([v[: rank * level, base : base + node] for v in vt], diag, nt=True)
            core = core_l[n][k]
            for ref, top, rest in zip(ch_refs[n], split(core), split(dot(gram, core))):
                ref[k, : 2 * rank] = top
                ref[k, 2 * rank :] = rest
    leaf_load.wait()
    high, low = split(leaf[...])
    a_high[:, :lf] = high
    a_low[:, :lf] = low
    for i in range(blocks):
        rows = slice(i * lf, (i + 1) * lf)
        high, low = split(
            dot3([v[:, rows] for v in vt], (a_high[rows, :lf], a_low[rows, :lf]))
        )
        m_high[i] = high
        m_low[i] = low

    first_copy, later_copy, q_copy, last_copy = {}, {}, {}, {}

    def forward(c):
        right_loads[c].wait()
        high, low = split(rbuf[c])
        r_high[c] = high
        r_low[c] = low
        parts = []
        for i in range(blocks):
            rows = slice(i * lf, (i + 1) * lf)
            parts.append(dot3((m_high[i], m_low[i]), (r_high[c, rows, :], r_low[c, rows, :])))
        for n in reversed(range(len(local_levels))):
            level = local_levels[n]
            top = rank * level
            merged = []
            for k in range(len(parts) // 2):
                a, b = parts[2 * k], parts[2 * k + 1]
                both = jnp.concatenate([b[top:], a[top:]], 0)
                image = dot3((ch_refs[n][0][k], ch_refs[n][1][k]), split(both))
                start = local_offset(level, bits, rank) + 2 * rank * k
                ql_ref[c, start : start + 2 * rank] = image[: 2 * rank]
                merged.append(a[:top] + b[:top] - image[2 * rank :])
            parts = merged
        p = parts[0]
        low, high = p[:, :LANES], p[:, LANES:]
        first_out[c, :rank] = low[:rank]
        first_out[c, rank : 2 * rank] = high[:rank]
        first_out[c, 2 * rank :] = jnp.where(upper, low[rank:], high[rank:])
        first_copy[c] = send(first_out.at[c], first_in.at[c], first_sem.at[c], 0)
        later_out[0, c] = jnp.where(upper, high[rank:], low[rank:])

    def bases():
        if local_levels:
            rows = [ut_ref[level] for level in local_levels]
            extra = a_high.shape[1] - lf - rank * len(rows)
            if extra:
                rows.append(jnp.zeros((extra, rows_dev), F32))
            high, low = split(-jnp.concatenate(rows, 0).T)
            a_high[:, lf:] = high
            a_low[:, lf:] = low
        rows = [ut_ref[bits - 1 - s] for s in range(bits)]
        extra = u_high.shape[1] - rank * bits
        if extra:
            rows.append(jnp.zeros((extra, rows_dev), F32))
        high, low = split(-jnp.concatenate(rows, 0).T)
        u_high[...] = high
        u_low[...] = low
        written.append(move(u_high, uh_hbm, sem_out, "out"))
        written.append(move(u_low, ul_hbm, sem_out, "out"))

    def leaves(c):
        for i in range(blocks):
            rows = slice(i * lf, (i + 1) * lf)
            highs, lows = [r_high[c, rows, :]], [r_low[c, rows, :]]
            width = lf
            for level in local_levels:
                place = rank * (i * 2 ** (level - bits + 1) // blocks)
                start = local_offset(level, bits, rank) + place
                high, low = split(ql_ref[c, start : start + rank])
                highs.append(high)
                lows.append(low)
                width += rank
            if a_high.shape[1] > width:
                zero = jnp.zeros((a_high.shape[1] - width, CHUNK), jnp.bfloat16)
                highs.append(zero)
                lows.append(zero)
            rbuf[c, rows, :] = dot3(
                (a_high[rows, :], a_low[rows, :]),
                (jnp.concatenate(highs, 0), jnp.concatenate(lows, 0)),
            )
        written.append(move(rbuf.at[c], x_hbm.at[:, pl.ds(c * CHUNK, CHUNK)], sem_out, "out"))

    def stack(mine, theirs, s):
        first = child(s) == 0
        return jnp.concatenate([jnp.where(first, theirs, mine), jnp.where(first, mine, theirs)], 0)

    def pick(image, s):
        first = child(s) == 0
        return (
            jnp.where(first, image[:rank], image[rank:]),
            jnp.where(first, image[rank:], image[:rank]),
        )

    def correction(s, own, sib):
        zeros = [jnp.zeros((rank, LANES), F32)]
        before, after = s, gram_cols // rank - 1 - s
        rows = slice(rank * s, None)
        q_own = jnp.concatenate(zeros * before + [own] + zeros * after, 0)
        q_sib = jnp.concatenate(zeros * before + [sib] + zeros * after, 0)
        return dot(gram_out[s, rows, :], q_own) + dot(gram_in[s, rows, :], q_sib)

    def grams(s):
        gram_copy[s].wait_recv()
        if s + 1 < bits - 1:
            gram_out[s + 1] = gram_out[s] + gram_in[s]
            gram_copy[s + 1] = send(
                gram_out.at[s + 1], gram_in.at[s + 1], gram_sem.at[s + 1], s + 1
            )

    def last_step(s, c):
        later_copy[s, c].wait_recv()
        last_copy[0].wait_recv()
        last_copy[1].wait_recv()
        live = slice(rank * (s - 1), rank * s)

        def join(here, there):
            return jnp.concatenate(
                [jnp.where(upper, there, here), jnp.where(upper, here, there)], 1
            )

        mine = join(later_out[s, c, live], last_in[0])
        theirs = join(later_in[s, c, live], last_in[1])
        last_q[...] = pick(dot(core_g[s], stack(mine, theirs, s)), s)[0]
        target = qg_hbm.at[pl.ds(s * rank, rank), pl.ds(c * CHUNK, CHUNK)]
        written.append(move(last_q, target, sem_out, "out"))

    def step(s, c):
        if c == 0:
            core_g_loads[s].wait()
        if s == bits - 1 and c == chunks - 1:
            last_step(s, c)
            return
        if s == 0:
            first_copy[c].wait_recv()
            mine = jnp.concatenate([first_out[c, :rank], first_out[c, rank : 2 * rank]], 1)
            theirs = jnp.concatenate([first_in[c, :rank], first_in[c, rank : 2 * rank]], 1)
            image = dot(core_g[0], stack(mine, theirs, 0))
            own, sib = pick(image, 0)
            q_first[c] = own
            own = jnp.where(upper, own[:, LANES:], own[:, :LANES])
            sib = jnp.where(upper, sib[:, LANES:], sib[:, :LANES])
            rest = later_out[0, c] + first_in[c, 2 * rank :]
        else:
            later_copy[s, c].wait_recv()
            live = slice(rank * (s - 1), rank * s)
            image = dot(core_g[s], stack(later_out[s, c, live], later_in[s, c, live], s))
            own, sib = pick(image, s)
            q_out[s - 1, c] = own
            start = pl.multiple_of(c * CHUNK + half_id * LANES, LANES)
            target = qg_hbm.at[pl.ds(s * rank, rank), pl.ds(start, LANES)]
            q_copy[s, c] = send(q_out.at[s - 1, c], target, q_sem.at[s - 1, c], 0)
            if s < bits - 1:
                rest = later_out[s, c, rank * s :] + later_in[s, c, rank * s :]
        if s < bits - 1:
            later_out[s + 1, c, rank * s :] = rest - correction(s, own, sib)
            if s == bits - 2 and c == chunks - 1:
                root = later_out.at[s + 1, c, pl.ds(rank * s, rank)]
                last_copy[1] = send(root, last_in.at[1], last_sem.at[1], None, cross)
                last_copy[0] = send(root, last_in.at[0], last_sem.at[0], 0)
            later_copy[s + 1, c] = send(
                later_out.at[s + 1, c, pl.ds(rank * s, rank * (bits - 1 - s))],
                later_in.at[s + 1, c, pl.ds(rank * s, rank * (bits - 1 - s))],
                later_sem.at[s, c],
                s + 1,
            )
        if s == 0:
            target = qg_hbm.at[pl.ds(0, rank), pl.ds(c * CHUNK, CHUNK)]
            written.append(move(q_first.at[c], target, sem_out, "out"))
        else:
            written.append(move(q_out.at[s - 1, c], target, sem_out, "out"))

    for c in range(chunks):
        forward(c)
        if c == 0:
            grams(0)
    for s in range(1, bits - 1):
        grams(s)
    bases()
    for t in range(chunks + bits - 1):
        for s in range(bits):
            c = t - s
            if 0 <= c < chunks:
                step(s, c)
        if t < chunks:
            leaves(t)
    for copy in q_copy.values():
        copy.wait_recv()
    for copy in written:
        copy.wait()
    for copy in sent:
        copy.wait_send()


def tree(bits, right_side, leaf_inverse, vt, ut, cores):
    rows_dev, cols = right_side.shape
    lf = leaf_inverse.shape[1]
    levels, rank = vt.shape[:2]
    blocks = rows_dev // lf
    chunks = cols // CHUNK
    local_levels = list(range(bits, levels))
    assert blocks == 2 ** len(local_levels) and bits >= 2
    gram_cols = pl.cdiv(rank * (bits - 1), LANES) * LANES
    depth = lf + pl.cdiv(rank * len(local_levels), LANES) * LANES
    wide = pl.cdiv(rank * bits, LANES) * LANES
    out_shape = [
        jax.ShapeDtypeStruct((rows_dev, cols), F32),
        jax.ShapeDtypeStruct((rank * bits, cols), F32),
        jax.ShapeDtypeStruct((rows_dev, wide), jnp.bfloat16),
        jax.ShapeDtypeStruct((rows_dev, wide), jnp.bfloat16),
    ]
    hbm = pl.BlockSpec(memory_space=pltpu.HBM)
    free = pl.BlockSpec(memory_space=pl.ANY)
    counts = [2 ** (level - bits) for level in local_levels]
    rest = rank * (bits - 1)
    half = jnp.bfloat16
    scratch = [
        pltpu.VMEM((chunks, rows_dev, CHUNK), F32),
        pltpu.VMEM((rows_dev, lf), F32),
        pltpu.VMEM((levels, rank, rows_dev), F32),
        pltpu.VMEM((levels, rank, rows_dev), F32),
        pltpu.VMEM((bits, 2 * rank, 2 * rank), F32),
        pltpu.SemaphoreType.DMA((3 + levels + chunks,)),
        pltpu.SemaphoreType.DMA((2 + chunks * (bits + 1),)),
        pltpu.VMEM((chunks, rows_dev, CHUNK), half),
        pltpu.VMEM((chunks, rows_dev, CHUNK), half),
        pltpu.VMEM((rows_dev, depth), half),
        pltpu.VMEM((rows_dev, depth), half),
        pltpu.VMEM((blocks, levels * rank, lf), half),
        pltpu.VMEM((blocks, levels * rank, lf), half),
        pltpu.VMEM((rows_dev, wide), half),
        pltpu.VMEM((rows_dev, wide), half),
        pltpu.VMEM((chunks, max(rank * (2 * blocks - 2), rank), CHUNK), F32),
        pltpu.VMEM((chunks, rank, CHUNK), F32),
        pltpu.VMEM((bits - 1, rest, gram_cols), F32),
        pltpu.VMEM((bits - 1, rest, gram_cols), F32),
        pltpu.VMEM((chunks, 2 * rank + rest, LANES), F32),
        pltpu.VMEM((chunks, 2 * rank + rest, LANES), F32),
        pltpu.VMEM((bits, chunks, rest, LANES), F32),
        pltpu.VMEM((bits, chunks, rest, LANES), F32),
        pltpu.VMEM((bits - 1, chunks, rank, LANES), F32),
        pltpu.SemaphoreType.DMA((bits - 1, 2)),
        pltpu.SemaphoreType.DMA((chunks, 2)),
        pltpu.SemaphoreType.DMA((bits - 1, chunks, 2)),
        pltpu.SemaphoreType.DMA((bits - 1, chunks, 2)),
        pltpu.VMEM((2, rank, LANES), F32),
        pltpu.VMEM((rank, CHUNK), F32),
        pltpu.SemaphoreType.DMA((2, 2)),
    ]
    scratch += [pltpu.VMEM((count, 2 * rank, 2 * rank), F32) for count in counts]
    scratch += [
        pltpu.VMEM((count, rank * (level + 2), 2 * rank), half)
        for count, level in zip(counts, local_levels)
        for _ in range(2)
    ]
    return pl.pallas_call(
        functools.partial(tree_kernel, bits, levels, blocks),
        out_shape=out_shape,
        in_specs=[hbm] * 5,
        out_specs=[free] * 4,
        scratch_shapes=scratch,
        compiler_params=pltpu.CompilerParams(
            collective_id=0, has_side_effects=True, vmem_limit_bytes=TREE_VMEM + 32 * rows_dev * lf
        ),
        name="tree",
    )(right_side, leaf_inverse, vt, ut, cores)


def apply_kernel(x_ref, uh_ref, ul_ref, q_ref, out_ref):
    pad = uh_ref.shape[1] - q_ref.shape[0]
    q = q_ref[...]
    if pad:
        q = jnp.concatenate([q, jnp.zeros((pad, q.shape[1]), F32)], 0)
    high, low = split(q)
    out_ref[...] = x_ref[...] + dot3((uh_ref[...], ul_ref[...]), (high, low))


def apply(x, q, u_high, u_low):
    rows_dev, cols = x.shape
    width = CHUNK

    def column(rows):
        return pl.BlockSpec((rows, width), lambda c: (0, c))

    whole = pl.BlockSpec(u_high.shape, lambda c: (0, 0))
    return pl.pallas_call(
        apply_kernel,
        grid=(cols // width,),
        out_shape=jax.ShapeDtypeStruct((rows_dev, cols), F32),
        in_specs=[column(rows_dev), whole, whole, column(q.shape[0])],
        out_specs=column(rows_dev),
        compiler_params=pltpu.CompilerParams(vmem_limit_bytes=APPLY_VMEM),
        name="apply",
    )(x, u_high, u_low, q)


def local(bits, right_side, leaf_inverse, left_factors, right_factors, cores):
    ut = jnp.swapaxes(left_factors, 1, 2)
    vt = jnp.swapaxes(right_factors, 1, 2)
    right_side, leaf_inverse, vt, ut, cores = (
        pltpu.with_memory_space_constraint(a, pltpu.HBM)
        for a in (right_side, leaf_inverse, vt, ut, cores)
    )
    x, q, u_high, u_low = tree(bits, right_side, leaf_inverse, vt, ut, cores)
    return apply(x, q, u_high, u_low)


def solution(mesh):
    bits = mesh.shape["rows"].bit_length() - 1
    in_specs = (
        P(("rep", "rows"), None),
        P(("rep", "rows"), None),
        P(None, ("rep", "rows"), None),
        P(None, ("rep", "rows"), None),
        P("rep", None, None),
    )
    out_specs = P(("rep", "rows"), None)
    return jax.shard_map(
        functools.partial(local, bits),
        mesh=mesh,
        in_specs=in_specs,
        out_specs=out_specs,
        check_vma=False,
    )
```

```python
import functools

import jax
import jax.numpy as jnp
from jax import lax
from jax.experimental import pallas as pl
from jax.experimental.pallas import tpu as pltpu
from jax.sharding import PartitionSpec as P

LANES = 128
CHUNK = 2 * LANES
F32 = jnp.float32
TREE_VMEM = 24 << 20
APPLY_VMEM = 12 << 20


def split(x):
    high = x.astype(jnp.bfloat16)
    return high, (x - high.astype(F32)).astype(jnp.bfloat16)


def level_order(bits, levels):
    return [bits - 1 - s for s in range(bits)] + list(range(bits, levels))


def local_offset(level, bits, rank):
    return rank * (2 ** (level - bits + 1) - 2)


def dot3(a, b, nt=False):
    dims = (((1,), (1 if nt else 0,)), ((), ()))

    def one(x, y):
        return lax.dot_general(x, y, dims, preferred_element_type=F32)

    return one(a[0], b[0]) + one(a[0], b[1]) + one(a[1], b[0])


def dot(a, b):
    return dot3(split(a), split(b))


def tree_kernel(bits, levels, blocks, right_hbm, leaf_hbm, vt_hbm, ut_hbm, cores_hbm, *refs):
    x_hbm, qg_hbm, uh_hbm, ul_hbm = refs[:4]
    rbuf, leaf, vt_ref, ut_ref, core_g, sem_in, sem_out = refs[4:11]
    r_high, r_low, a_high, a_low, m_high, m_low, u_high, u_low, ql_ref, q_first = refs[11:21]
    gram_out, gram_in, first_out, first_in, later_out, later_in, q_out = refs[21:28]
    gram_sem, first_sem, later_sem, q_sem = refs[28:32]
    last_in, last_q, last_sem = refs[32:35]
    local_levels = list(range(bits, levels))
    core_l = refs[35 : 35 + len(local_levels)]
    ch_refs = refs[35 + len(local_levels) :]
    ch_refs = list(zip(ch_refs[::2], ch_refs[1::2]))

    me = lax.axis_index("rows")
    rank, rows_dev = vt_ref.shape[1:]
    chunks = rbuf.shape[0]
    lf = rows_dev // blocks
    half_id = lax.rem(me, 2)
    upper = half_id == 1
    order = level_order(bits, levels)

    def child(s):
        return lax.rem(me // 2**s, 2)

    def partner(s):
        return me + (1 - 2 * child(s)) * 2**s

    cross = partner(bits - 1) + (1 - 2 * child(0))
    barrier = pltpu.get_barrier_semaphore()
    for target in [partner(s) for s in range(bits)] + [cross]:
        pl.semaphore_signal(
            barrier, inc=1, device_id={"rows": target}, device_id_type=pl.DeviceIdType.MESH
        )

    slots = {"in": 0, "out": 0}

    def move(src, dst, sems, kind):
        copy = pltpu.make_async_copy(src, dst, sems.at[slots[kind]])
        slots[kind] += 1
        copy.start()
        return copy

    factor_loads = [move(vt_hbm, vt_ref, sem_in, "in"), move(ut_hbm, ut_ref, sem_in, "in")]
    leaf_load = move(leaf_hbm, leaf, sem_in, "in")
    core_loads = []
    for n, level in enumerate(local_levels):
        count = 2 ** (level - bits)
        src = cores_hbm.at[pl.ds(2**level - 1 + me * count, count)]
        core_loads.append(move(src, core_l[n], sem_in, "in"))
    right_loads = [
        move(right_hbm.at[:, pl.ds(c * CHUNK, CHUNK)], rbuf.at[c], sem_in, "in")
        for c in range(chunks)
    ]
    core_g_loads = []
    for s in range(bits):
        src = cores_hbm.at[2 ** (bits - 1 - s) - 1 + me // 2 ** (s + 1)]
        core_g_loads.append(move(src, core_g.at[s], sem_in, "in"))

    sent, written = [], []

    def send(src, dst, sems, s, target=None):
        copy = pltpu.make_async_remote_copy(
            src_ref=src,
            dst_ref=dst,
            send_sem=sems.at[0],
            recv_sem=sems.at[1],
            device_id={"rows": partner(s) if target is None else target},
            device_id_type=pl.DeviceIdType.MESH,
        )
        copy.start()
        sent.append(copy)
        return copy

    for copy in factor_loads:
        copy.wait()
    gram_cols = gram_out.shape[2]
    vt = split(jnp.concatenate([vt_ref[level] for level in order], 0))
    ut = split(jnp.concatenate([ut_ref[level] for level in order], 0))
    v_rows = [v[rank : rank * bits] for v in vt]
    u_rows = [u[:gram_cols] for u in ut]
    gram_out[0] = dot3(v_rows, u_rows, nt=True)
    pl.semaphore_wait(barrier, bits + 1)
    gram_copy = {0: send(gram_out.at[0], gram_in.at[0], gram_sem.at[0], 0)}

    for copy in core_loads:
        copy.wait()
    for n, level in enumerate(local_levels):
        count = 2 ** (level - bits)
        node = rows_dev // count
        half = node // 2
        zero = jnp.zeros((rank, half), jnp.bfloat16)
        own = slice(rank * level, rank * (level + 1))
        for k in range(count):
            base = k * node
            diag = [
                jnp.concatenate(
                    [
                        jnp.concatenate([u[own, base : base + half], zero], 1),
                        jnp.concatenate([zero, u[own, base + half : base + node]], 1),
                    ],
                    0,
                )
                for u in ut
            ]
            gram = dot3([v[: rank * level, base : base + node] for v in vt], diag, nt=True)
            core = core_l[n][k]
            for ref, top, rest in zip(ch_refs[n], split(core), split(dot(gram, core))):
                ref[k, : 2 * rank] = top
                ref[k, 2 * rank :] = rest
    leaf_load.wait()
    high, low = split(leaf[...])
    a_high[:, :lf] = high
    a_low[:, :lf] = low
    for i in range(blocks):
        rows = slice(i * lf, (i + 1) * lf)
        high, low = split(
            dot3([v[:, rows] for v in vt], (a_high[rows, :lf], a_low[rows, :lf]))
        )
        m_high[i] = high
        m_low[i] = low

    first_copy, later_copy, q_copy, last_copy = {}, {}, {}, {}

    def forward(c):
        right_loads[c].wait()
        high, low = split(rbuf[c])
        r_high[c] = high
        r_low[c] = low
        parts, later = [], []
        for i in range(blocks):
            rows = slice(i * lf, (i + 1) * lf)
            parts.append(dot3((m_high[i], m_low[i]), (r_high[c, rows, :], r_low[c, rows, :])))
        for n in reversed(range(len(local_levels))):
            level = local_levels[n]
            top = rank * level
            merged = []
            for k in range(len(parts) // 2):
                a, b = parts[2 * k], parts[2 * k + 1]
                both = split(jnp.concatenate([b[top:], a[top:]], 0))
                change = dot3([ref[k, 2 * rank :] for ref in ch_refs[n]], both)
                start = local_offset(level, bits, rank) + 2 * rank * k
                later.append((start, n, k, both))
                merged.append(a[:top] + b[:top] - change)
            parts = merged
        p = parts[0]
        low, high = p[:, :LANES], p[:, LANES:]
        first_out[c, :rank] = low[:rank]
        first_out[c, rank : 2 * rank] = high[:rank]
        first_out[c, 2 * rank :] = jnp.where(upper, low[rank:], high[rank:])
        first_copy[c] = send(first_out.at[c], first_in.at[c], first_sem.at[c], 0)
        later_out[0, c] = jnp.where(upper, high[rank:], low[rank:])
        for start, n, k, both in later:
            ql_ref[c, start : start + 2 * rank] = dot3(
                [ref[k, : 2 * rank] for ref in ch_refs[n]], both
            )

    def bases():
        if local_levels:
            rows = [ut_ref[level] for level in local_levels]
            extra = a_high.shape[1] - lf - rank * len(rows)
            if extra:
                rows.append(jnp.zeros((extra, rows_dev), F32))
            high, low = split(-jnp.concatenate(rows, 0).T)
            a_high[:, lf:] = high
            a_low[:, lf:] = low
        rows = [ut_ref[bits - 1 - s] for s in range(bits)]
        extra = u_high.shape[1] - rank * bits
        if extra:
            rows.append(jnp.zeros((extra, rows_dev), F32))
        high, low = split(-jnp.concatenate(rows, 0).T)
        u_high[...] = high
        u_low[...] = low
        written.append(move(u_high, uh_hbm, sem_out, "out"))
        written.append(move(u_low, ul_hbm, sem_out, "out"))

    def leaves(c):
        for i in range(blocks):
            rows = slice(i * lf, (i + 1) * lf)
            highs, lows = [r_high[c, rows, :]], [r_low[c, rows, :]]
            width = lf
            for level in local_levels:
                place = rank * (i * 2 ** (level - bits + 1) // blocks)
                start = local_offset(level, bits, rank) + place
                high, low = split(ql_ref[c, start : start + rank])
                highs.append(high)
                lows.append(low)
                width += rank
            if a_high.shape[1] > width:
                zero = jnp.zeros((a_high.shape[1] - width, CHUNK), jnp.bfloat16)
                highs.append(zero)
                lows.append(zero)
            rbuf[c, rows, :] = dot3(
                (a_high[rows, :], a_low[rows, :]),
                (jnp.concatenate(highs, 0), jnp.concatenate(lows, 0)),
            )
        written.append(move(rbuf.at[c], x_hbm.at[:, pl.ds(c * CHUNK, CHUNK)], sem_out, "out"))

    def stack(mine, theirs, s):
        first = child(s) == 0
        return jnp.concatenate([jnp.where(first, theirs, mine), jnp.where(first, mine, theirs)], 0)

    def pick(image, s):
        first = child(s) == 0
        return (
            jnp.where(first, image[:rank], image[rank:]),
            jnp.where(first, image[rank:], image[:rank]),
        )

    def correction(s, own, sib):
        zeros = [jnp.zeros((rank, LANES), F32)]
        before, after = s, gram_cols // rank - 1 - s
        rows = slice(rank * s, None)
        q_own = jnp.concatenate(zeros * before + [own] + zeros * after, 0)
        q_sib = jnp.concatenate(zeros * before + [sib] + zeros * after, 0)
        return dot(gram_out[s, rows, :], q_own) + dot(gram_in[s, rows, :], q_sib)

    def grams(s):
        gram_copy[s].wait_recv()
        if s + 1 < bits - 1:
            gram_out[s + 1] = gram_out[s] + gram_in[s]
            gram_copy[s + 1] = send(
                gram_out.at[s + 1], gram_in.at[s + 1], gram_sem.at[s + 1], s + 1
            )

    def last_step(s, c):
        later_copy[s, c].wait_recv()
        last_copy[0].wait_recv()
        last_copy[1].wait_recv()
        live = slice(rank * (s - 1), rank * s)

        def join(here, there):
            return jnp.concatenate(
                [jnp.where(upper, there, here), jnp.where(upper, here, there)], 1
            )

        mine = join(later_out[s, c, live], last_in[0])
        theirs = join(later_in[s, c, live], last_in[1])
        last_q[...] = pick(dot(core_g[s], stack(mine, theirs, s)), s)[0]
        target = qg_hbm.at[pl.ds(s * rank, rank), pl.ds(c * CHUNK, CHUNK)]
        written.append(move(last_q, target, sem_out, "out"))

    def step(s, c):
        if c == 0:
            core_g_loads[s].wait()
        if s == bits - 1 and c == chunks - 1:
            last_step(s, c)
            return
        if s == 0:
            first_copy[c].wait_recv()
            mine = jnp.concatenate([first_out[c, :rank], first_out[c, rank : 2 * rank]], 1)
            theirs = jnp.concatenate([first_in[c, :rank], first_in[c, rank : 2 * rank]], 1)
            image = dot(core_g[0], stack(mine, theirs, 0))
            own, sib = pick(image, 0)
            q_first[c] = own
            own = jnp.where(upper, own[:, LANES:], own[:, :LANES])
            sib = jnp.where(upper, sib[:, LANES:], sib[:, :LANES])
            rest = later_out[0, c] + first_in[c, 2 * rank :]
        else:
            later_copy[s, c].wait_recv()
            live = slice(rank * (s - 1), rank * s)
            image = dot(core_g[s], stack(later_out[s, c, live], later_in[s, c, live], s))
            own, sib = pick(image, s)
            q_out[s - 1, c] = own
            start = pl.multiple_of(c * CHUNK + half_id * LANES, LANES)
            target = qg_hbm.at[pl.ds(s * rank, rank), pl.ds(start, LANES)]
            q_copy[s, c] = send(q_out.at[s - 1, c], target, q_sem.at[s - 1, c], 0)
            if s < bits - 1:
                rest = later_out[s, c, rank * s :] + later_in[s, c, rank * s :]
        if s < bits - 1:
            later_out[s + 1, c, rank * s :] = rest - correction(s, own, sib)
            if s == bits - 2 and c == chunks - 1:
                root = later_out.at[s + 1, c, pl.ds(rank * s, rank)]
                last_copy[1] = send(root, last_in.at[1], last_sem.at[1], None, cross)
                last_copy[0] = send(root, last_in.at[0], last_sem.at[0], 0)
            later_copy[s + 1, c] = send(
                later_out.at[s + 1, c, pl.ds(rank * s, rank * (bits - 1 - s))],
                later_in.at[s + 1, c, pl.ds(rank * s, rank * (bits - 1 - s))],
                later_sem.at[s, c],
                s + 1,
            )
        if s == 0:
            target = qg_hbm.at[pl.ds(0, rank), pl.ds(c * CHUNK, CHUNK)]
            written.append(move(q_first.at[c], target, sem_out, "out"))
        else:
            written.append(move(q_out.at[s - 1, c], target, sem_out, "out"))

    for c in range(chunks):
        forward(c)
        if c == 0:
            grams(0)
    for s in range(1, bits - 1):
        grams(s)
    bases()
    for t in range(chunks + bits - 1):
        for s in range(bits):
            c = t - s
            if 0 <= c < chunks:
                step(s, c)
        if t < chunks:
            leaves(t)
    for copy in q_copy.values():
        copy.wait_recv()
    for copy in written:
        copy.wait()
    for copy in sent:
        copy.wait_send()


def tree(bits, right_side, leaf_inverse, vt, ut, cores):
    rows_dev, cols = right_side.shape
    lf = leaf_inverse.shape[1]
    levels, rank = vt.shape[:2]
    blocks = rows_dev // lf
    chunks = cols // CHUNK
    local_levels = list(range(bits, levels))
    assert blocks == 2 ** len(local_levels) and bits >= 2
    gram_cols = pl.cdiv(rank * (bits - 1), LANES) * LANES
    depth = lf + pl.cdiv(rank * len(local_levels), LANES) * LANES
    wide = pl.cdiv(rank * bits, LANES) * LANES
    out_shape = [
        jax.ShapeDtypeStruct((rows_dev, cols), F32),
        jax.ShapeDtypeStruct((rank * bits, cols), F32),
        jax.ShapeDtypeStruct((rows_dev, wide), jnp.bfloat16),
        jax.ShapeDtypeStruct((rows_dev, wide), jnp.bfloat16),
    ]
    hbm = pl.BlockSpec(memory_space=pltpu.HBM)
    free = pl.BlockSpec(memory_space=pl.ANY)
    counts = [2 ** (level - bits) for level in local_levels]
    rest = rank * (bits - 1)
    half = jnp.bfloat16
    scratch = [
        pltpu.VMEM((chunks, rows_dev, CHUNK), F32),
        pltpu.VMEM((rows_dev, lf), F32),
        pltpu.VMEM((levels, rank, rows_dev), F32),
        pltpu.VMEM((levels, rank, rows_dev), F32),
        pltpu.VMEM((bits, 2 * rank, 2 * rank), F32),
        pltpu.SemaphoreType.DMA((3 + levels + chunks,)),
        pltpu.SemaphoreType.DMA((2 + chunks * (bits + 1),)),
        pltpu.VMEM((chunks, rows_dev, CHUNK), half),
        pltpu.VMEM((chunks, rows_dev, CHUNK), half),
        pltpu.VMEM((rows_dev, depth), half),
        pltpu.VMEM((rows_dev, depth), half),
        pltpu.VMEM((blocks, levels * rank, lf), half),
        pltpu.VMEM((blocks, levels * rank, lf), half),
        pltpu.VMEM((rows_dev, wide), half),
        pltpu.VMEM((rows_dev, wide), half),
        pltpu.VMEM((chunks, max(rank * (2 * blocks - 2), rank), CHUNK), F32),
        pltpu.VMEM((chunks, rank, CHUNK), F32),
        pltpu.VMEM((bits - 1, rest, gram_cols), F32),
        pltpu.VMEM((bits - 1, rest, gram_cols), F32),
        pltpu.VMEM((chunks, 2 * rank + rest, LANES), F32),
        pltpu.VMEM((chunks, 2 * rank + rest, LANES), F32),
        pltpu.VMEM((bits, chunks, rest, LANES), F32),
        pltpu.VMEM((bits, chunks, rest, LANES), F32),
        pltpu.VMEM((bits - 1, chunks, rank, LANES), F32),
        pltpu.SemaphoreType.DMA((bits - 1, 2)),
        pltpu.SemaphoreType.DMA((chunks, 2)),
        pltpu.SemaphoreType.DMA((bits - 1, chunks, 2)),
        pltpu.SemaphoreType.DMA((bits - 1, chunks, 2)),
        pltpu.VMEM((2, rank, LANES), F32),
        pltpu.VMEM((rank, CHUNK), F32),
        pltpu.SemaphoreType.DMA((2, 2)),
    ]
    scratch += [pltpu.VMEM((count, 2 * rank, 2 * rank), F32) for count in counts]
    scratch += [
        pltpu.VMEM((count, rank * (level + 2), 2 * rank), half)
        for count, level in zip(counts, local_levels)
        for _ in range(2)
    ]
    return pl.pallas_call(
        functools.partial(tree_kernel, bits, levels, blocks),
        out_shape=out_shape,
        in_specs=[hbm] * 5,
        out_specs=[free] * 4,
        scratch_shapes=scratch,
        compiler_params=pltpu.CompilerParams(
            collective_id=0, has_side_effects=True, vmem_limit_bytes=TREE_VMEM + 32 * rows_dev * lf
        ),
        name="tree",
    )(right_side, leaf_inverse, vt, ut, cores)


def apply_kernel(x_ref, uh_ref, ul_ref, q_ref, out_ref):
    pad = uh_ref.shape[1] - q_ref.shape[0]
    q = q_ref[...]
    if pad:
        q = jnp.concatenate([q, jnp.zeros((pad, q.shape[1]), F32)], 0)
    high, low = split(q)
    out_ref[...] = x_ref[...] + dot3((uh_ref[...], ul_ref[...]), (high, low))


def apply(x, q, u_high, u_low):
    rows_dev, cols = x.shape
    width = CHUNK

    def column(rows):
        return pl.BlockSpec((rows, width), lambda c: (0, c))

    whole = pl.BlockSpec(u_high.shape, lambda c: (0, 0))
    return pl.pallas_call(
        apply_kernel,
        grid=(cols // width,),
        out_shape=jax.ShapeDtypeStruct((rows_dev, cols), F32),
        in_specs=[column(rows_dev), whole, whole, column(q.shape[0])],
        out_specs=column(rows_dev),
        compiler_params=pltpu.CompilerParams(vmem_limit_bytes=APPLY_VMEM),
        name="apply",
    )(x, u_high, u_low, q)


def local(bits, right_side, leaf_inverse, left_factors, right_factors, cores):
    ut = jnp.swapaxes(left_factors, 1, 2)
    vt = jnp.swapaxes(right_factors, 1, 2)
    right_side, leaf_inverse, vt, ut, cores = (
        pltpu.with_memory_space_constraint(a, pltpu.HBM)
        for a in (right_side, leaf_inverse, vt, ut, cores)
    )
    x, q, u_high, u_low = tree(bits, right_side, leaf_inverse, vt, ut, cores)
    return apply(x, q, u_high, u_low)


def solution(mesh):
    bits = mesh.shape["rows"].bit_length() - 1
    in_specs = (
        P(("rep", "rows"), None),
        P(("rep", "rows"), None),
        P(None, ("rep", "rows"), None),
        P(None, ("rep", "rows"), None),
        P("rep", None, None),
    )
    out_specs = P(("rep", "rows"), None)
    return jax.shard_map(
        functools.partial(local, bits),
        mesh=mesh,
        in_specs=in_specs,
        out_specs=out_specs,
        check_vma=False,
    )
```
